512 devices in a mesh: tm: 8 (over y, core), net: 16 (over z), cols: 4 (over x).
Axes of the slice: x: 4, y: 4, z: 16, core: 2. Of those that a mesh axis runs over, the one named last changes fastest.
Arguments:
- jac: bfloat16 [16, 64, 3, 128, 128], P('tm', 'net'), may hold values from -0.5 to 1.5
- block_cols: int32 [64, 2], P('net'), may hold values from 0 to 3
- iface_jac: bfloat16 [16, 16, 16, 128, 128], P('tm', 'net'), may hold values from -0.1796875 to 0.1796875
- iface_send: int32 [16, 16], P('net'), may hold values from 0 to 3
- iface_recv: int32 [16, 16], P('net'), may hold values from 0 to 3
- iface_live: int32 [16, 16], P('net'), may hold values from 0 to 128
- ctrl_node: int32 [768], P('cols'), may hold values from 0 to 8191
- ctrl_gain: float32 [16, 768], P('tm', 'cols'), may hold values from -6 to 6
Outputs:
- sens: bfloat16 [16, 768, 8192], P('tm', 'cols', 'net')
The draws below stay inside these ranges and needn't reach their ends.
All inputs are finite; a program needn't handle non-finite values.
Results may differ from the reference program's by a relative error of at most 0.013.
Values may be sent and summed in bfloat16 or wider, within the bound.
A program may use at most 64 MiB of HBM per device.

```python
import math
import jax
import jax.numpy as jnp
from jax import lax

BLK = 128
NB = 4
K = 3
CTRL = 768
BLOCKS = 64
NSTATES = 8192
HORIZON = 16
N_NET = 16


def draw_jac(key, part):
    shape = (HORIZON, BLOCKS, K, BLK, BLK)
    spread = 0.2 / math.sqrt(BLK * K)
    noise = jax.random.normal(key, shape, jnp.float32) * spread
    keeping = jnp.exp(jax.random.uniform(jax.random.fold_in(key, 11), (BLOCKS, BLK), jnp.float32, math.log(0.55), math.log(0.995)))
    unit = jnp.eye(BLK, dtype=jnp.float32)
    leading = (jnp.arange(K) == 0).astype(jnp.float32)
    diagonal = keeping[None, :, None, :, None] * unit[None, None, None] * leading[None, None, :, None, None]
    return (noise + diagonal).astype(jnp.bfloat16)


def place_ends(values, stream_key, low, top_value):
    spot = [jax.random.randint(jax.random.fold_in(stream_key, axis), (), 0, length) for axis, length in enumerate(values.shape)]
    main_axis = values.shape.index(max(values.shape))
    neighbour = spot[:main_axis] + [(spot[main_axis] + 1) % values.shape[main_axis]] + spot[main_axis + 1:]
    return values.at[tuple(spot)].set(low).at[tuple(neighbour)].set(top_value)


def shard_levels(rng, dims, shards, low, top_value):
    loudness = 1.0
    for dim, parts in shards:
        draws = jax.random.uniform(jax.random.fold_in(jax.random.fold_in(rng, 6), dim), (parts,), jnp.float32, low / len(shards), top_value / len(shards))
        loudness = loudness * jnp.repeat(jnp.exp(draws), dims[dim] // parts).reshape((-1,) + (1,) * (len(dims) - 1 - dim))
    return loudness


def centred(own_key, shape, deviation, bound, cuts=(), kind=jnp.bfloat16):
    drawn = jax.random.normal(own_key, shape, jnp.float32) * deviation
    if len(cuts) > 0:
        drawn = shard_levels(own_key, shape, cuts, -0.22, 0.18) * drawn
    return jnp.clip(drawn, min=-bound, max=bound).astype(kind)


def setup_inputs(seed: int = 0) -> dict:
    seeds = jax.random.split(jax.random.key(seed), 9)
    jac = draw_jac(jax.random.fold_in(seeds[8], 71), 0)
    block_cols = place_ends(jax.random.randint(seeds[1], (BLOCKS, K - 1), 0, NB), jax.random.fold_in(seeds[1], 1), 0, NB - 1).astype(jnp.int32)
    iface_jac = centred(seeds[2], (HORIZON, N_NET, N_NET, BLK, BLK), 0.03, 0.1796875, ((0, 8), (1, 16)))
    iface_send = place_ends(jax.random.randint(seeds[3], (N_NET, N_NET), 0, NB), jax.random.fold_in(seeds[3], 1), 0, NB - 1).astype(jnp.int32)
    iface_recv = place_ends(jax.random.randint(seeds[4], (N_NET, N_NET), 0, NB), jax.random.fold_in(seeds[4], 1), 0, NB - 1).astype(jnp.int32)
    iface_live = place_ends(jax.random.randint(seeds[5], (N_NET, N_NET), 0, BLK + 1), jax.random.fold_in(seeds[5], 1), 0, BLK).astype(jnp.int32)
    ctrl_node = place_ends(jax.random.randint(seeds[6], (CTRL,), 0, NSTATES), jax.random.fold_in(seeds[6], 1), 0, NSTATES - 1).astype(jnp.int32)
    ctrl_gain = centred(seeds[7], (HORIZON, CTRL), 1.0, 6.0, ((0, 8), (1, 4)), jnp.float32)
    return dict(jac=jac, block_cols=block_cols, iface_jac=iface_jac, iface_send=iface_send, iface_recv=iface_recv, iface_live=iface_live, ctrl_node=ctrl_node, ctrl_gain=ctrl_gain)


def reference(jac, block_cols, iface_jac, iface_send, iface_recv, iface_live, ctrl_node, ctrl_gain):
    block_count = N_NET * NB
    state_count = block_count * BLK
    partition = jnp.arange(block_count, dtype=jnp.int32) // NB
    near_blocks = (partition[:, None] * NB + block_cols).astype(jnp.int32)
    senders = jnp.arange(N_NET, dtype=jnp.int32)
    send_blocks = (senders[None, :] * NB + iface_send.T).astype(jnp.int32)
    recv_blocks = (senders[:, None] * NB + iface_recv).astype(jnp.int32)
    live_mask = (jnp.arange(BLK, dtype=jnp.int32)[None, None, :] < iface_live[:, :, None]).astype(jnp.float32)
    receive_map = (recv_blocks[:, :, None] == jnp.arange(block_count, dtype=jnp.int32)[None, None, :]).astype(jnp.float32)
    placed = (ctrl_node[:, None] == jnp.arange(state_count, dtype=jnp.int32)[None, :]).astype(jnp.float32)
    highest = lax.Precision.HIGHEST

    def advance(state, inputs):
        step_jac, step_iface, gain_row = inputs
        state_tiles = state.astype(jnp.float32).reshape(CTRL, block_count, BLK)
        dense = step_jac.astype(jnp.float32)
        summed = jnp.einsum('iab,cib->cia', dense[:, 0], state_tiles, precision=highest)
        near_tiles = state_tiles[:, near_blocks, :]
        summed = summed + jnp.einsum('ikab,cikb->cia', dense[:, 1:], near_tiles, precision=highest)
        sources = state_tiles[:, send_blocks, :]
        coupled = jnp.einsum('pqab,cpqb->cpqa', step_iface.astype(jnp.float32), sources, precision=highest)
        coupled = coupled * live_mask[None]
        summed = summed + jnp.einsum('cpqa,pqi->cia', coupled, receive_map, precision=highest)
        total = summed.reshape(CTRL, state_count) + gain_row[:, None] * placed
        new_state = total.astype(jnp.bfloat16)
        return new_state, new_state

    initial = jnp.zeros((CTRL, state_count), jnp.bfloat16)
    final_state, produced = lax.scan(advance, initial, (jac, iface_jac, ctrl_gain))
    return produced
```

```python
import jax
import jax.numpy as jnp
from jax import lax
from jax.experimental import pallas as pl
from jax.experimental.pallas import tpu as pltpu
from jax.sharding import PartitionSpec as P

MESH = pl.DeviceIdType.MESH
TM = 8
NET = 16
COLS = 4
NB = 4
BLK = 128
STEPS = 16
WIDE = 192
W = WIDE // TM
Q = NET // COLS
NEAR = sorted(range(1, NET), key=lambda d: min(d, NET - d))
FAR = NEAR[::-1]


def dot_t(x, w):
    return lax.dot_general(
        x, w, (((1,), (1,)), ((), ())), preferred_element_type=jnp.float32
    )


def kernel(
    jac, iface, bcols, send, recv, live, node, gain, out,
    ja, ia, gains, state, zero, wide, wide_out, stage, sbuf, rbuf,
    own_sem, quarter_sem, sib_sem, ysend, sibsend, xsend,
    gain_send, gain_recv, first_send, first_recv,
    ex_send, ex_recv, out_send, out_recv,
):
    tm = lax.axis_index("tm")
    me = lax.axis_index("net")
    x = lax.axis_index("cols")
    y, core = tm // 2, lax.rem(tm, 2)
    sibling = 2 * y + 1 - core
    lane = lax.broadcasted_iota(jnp.int32, (1, BLK), 1)

    def remote(src, dst, ssem, rsem, **device):
        return pltpu.make_async_remote_copy(
            src_ref=src, dst_ref=dst, send_sem=ssem, recv_sem=rsem,
            device_id=device, device_id_type=MESH,
        )

    def wait(ref, sem):
        pltpu.make_async_copy(ref, ref, sem).wait()

    barrier = pltpu.get_barrier_semaphore()
    for d in FAR:
        pl.semaphore_signal(barrier, inc=1, device_id={"net": lax.rem(me + d, NET)}, device_id_type=MESH)
    for d in range(1, TM):
        pl.semaphore_signal(barrier, inc=1, device_id={"tm": lax.rem(tm + d, TM)}, device_id_type=MESH)
    for d in range(1, COLS):
        pl.semaphore_signal(barrier, inc=1, device_id={"cols": lax.rem(x + d, COLS)}, device_id_type=MESH)

    own = []
    for s in range(2):
        own.append(pltpu.make_async_copy(jac.at[s], ja.at[2 * tm + s], own_sem.at[s, 0]))
        own.append(pltpu.make_async_copy(iface.at[s], ia.at[2 * tm + s], own_sem.at[s, 1]))
    for copy in own:
        copy.start()

    def near_terms(t, ref):
        sums = []
        for i in range(NB):
            values = jnp.concatenate([ref[i], ref[bcols[i, 0]], ref[bcols[i, 1]]], axis=1)
            weights = jnp.concatenate([ja[t, i, 0], ja[t, i, 1], ja[t, i, 2]], axis=1)
            sums.append(dot_t(values, weights))
        return sums

    def add_interface(sums, t, q, values):
        term = dot_t(values, ia[t, q])
        reach, block = live[0, q], recv[0, q]
        return [
            total + jnp.where(lane < jnp.where(block == i, reach, 0), term, 0.0)
            for i, total in enumerate(sums)
        ]

    def inject(total, i, nodes, gain_rows):
        return total + jnp.where(nodes == lane + (me * NB + i) * BLK, gain_rows, 0.0)

    for copy in own:
        copy.wait()
    gains[pl.ds(2 * tm, 2)] = gain[tm]

    @pl.when(tm == 0)
    def _():
        zero[...] = jnp.zeros_like(zero)
        sums = near_terms(0, zero)
        for q in range(NET):
            sums = add_interface(sums, 0, q, zero[0])
        for i in range(NB):
            for g in range(TM):
                rows = sums[i][g * W : (g + 1) * W]
                new = inject(rows, i, node[g], gain[g, 0]).astype(jnp.bfloat16)
                wide[g, i] = new
                wide_out[g, :, i * BLK : (i + 1) * BLK] = new
        pltpu.make_async_copy(wide_out, out.at[0], out_recv.at[0, 0]).start()
        state[...] = wide[0]

    pl.semaphore_wait(barrier, NET - 1 + TM - 1 + COLS - 1)

    @pl.when(tm == 0)
    def _():
        for g in range(1, TM):
            remote(wide.at[g], state, first_send.at[g], first_recv, tm=g).start()

    def j_part(t, k):
        return ja.at[t, k]

    def i_part(t, k):
        return ia.at[t, pl.ds(k * Q, Q)]

    def spread_own(s):
        t = 2 * tm + s
        for d in range(1, 4):
            there = 2 * lax.rem(y + d, 4) + core
            remote(jac.at[s, x], j_part(t, x), ysend.at[s, 0], quarter_sem.at[t, x, 0], tm=there).start()
            remote(iface.at[s, pl.ds(x * Q, Q)], i_part(t, x), ysend.at[s, 1], quarter_sem.at[t, x, 1], tm=there).start()
        remote(jac.at[s], ja.at[t], sibsend.at[t, 0], sib_sem.at[t, 0], tm=sibling).start()
        remote(iface.at[s], ia.at[t], sibsend.at[t, 1], sib_sem.at[t, 1], tm=sibling).start()

    def to_sibling(t, k):
        remote(j_part(t, k), j_part(t, k), sibsend.at[t, 0], sib_sem.at[t, 0], tm=sibling).start()
        remote(i_part(t, k), i_part(t, k), sibsend.at[t, 1], sib_sem.at[t, 1], tm=sibling).start()

    def forwards(t):
        return jnp.logical_and(
            t < STEPS, jnp.logical_and(lax.rem(t // 2, 2) == core, t // 4 != y)
        )

    def forward_own_quarter(t):
        @pl.when(forwards(t))
        def _():
            wait(j_part(t, x), quarter_sem.at[t, x, 0])
            wait(i_part(t, x), quarter_sem.at[t, x, 1])
            for d in range(1, COLS):
                there = lax.rem(x + d, COLS)
                remote(j_part(t, x), j_part(t, x), xsend.at[t, 0], quarter_sem.at[t, x, 0], cols=there).start()
                remote(i_part(t, x), i_part(t, x), xsend.at[t, 1], quarter_sem.at[t, x, 1], cols=there).start()
            to_sibling(t, x)

    def forward_other_quarters(t):
        @pl.when(forwards(t))
        def _():
            for d in range(1, COLS):
                k = lax.rem(x + d, COLS)
                wait(j_part(t, k), quarter_sem.at[t, k, 0])
                wait(i_part(t, k), quarter_sem.at[t, k, 1])
                to_sibling(t, k)

    def from_sibling(t):
        @pl.when(lax.rem(t // 2, 2) != core)
        def _():
            wait(ja.at[t], sib_sem.at[t, 0])
            wait(ia.at[t], sib_sem.at[t, 1])

    @pl.when(y == 0)
    def _():
        @pl.when(tm != 0)
        def _():
            spread_own(0)

        spread_own(1)

    for d in range(1, TM):
        there = lax.rem(tm + d, TM)
        remote(gain.at[there], gains.at[pl.ds(2 * tm, 2)], gain_send.at[d], gain_recv.at[d], tm=there).start()

    @pl.when(tm != 0)
    def _():
        wait(state, first_recv)

    def exchange(t):
        slot = lax.rem(t, 2)
        for d in FAR:
            p = lax.rem(me + d, NET)
            sbuf[slot, d] = state[send[0, p]]
            remote(sbuf.at[slot, d], rbuf.at[slot, d], ex_send.at[slot, d], ex_recv.at[slot, d], net=p).start()

    def step(t, carry):
        slot = lax.rem(t, 2)
        exchange(t)

        @pl.when(t == 1)
        def _():
            forward_own_quarter(1)
            forward_own_quarter(2)
            forward_other_quarters(1)

        @pl.when(jnp.logical_and(y > 0, t == jnp.maximum(4 * y - 4, 1)))
        def _():
            spread_own(0)
            spread_own(1)

        forward_own_quarter(t + 2)
        forward_other_quarters(t + 1)
        from_sibling(t)

        @pl.when(t == 1)
        def _():
            for d in range(1, TM):
                source = lax.rem(tm - d + TM, TM)
                wait(gains.at[pl.ds(2 * source, 2)], gain_recv.at[d])

        sums = near_terms(t, state)
        sums = add_interface(sums, t, me, state[send[0, me]])
        for d in NEAR:
            wait(rbuf.at[slot, d], ex_recv.at[slot, d])
            sums = add_interface(sums, t, lax.rem(me - d + NET, NET), rbuf[slot, d])
        nodes, gain_rows = node[tm], gains[t]
        for i in range(NB):
            new = inject(sums[i], i, nodes, gain_rows).astype(jnp.bfloat16)
            state[i] = new
            stage[t, :, i * BLK : (i + 1) * BLK] = new

        there, s = t // 2, lax.rem(t, 2)

        @pl.when(there == tm)
        def _():
            pltpu.make_async_copy(stage.at[t], out.at[s, tm], out_recv.at[s, tm]).start()

        @pl.when(there != tm)
        def _():
            remote(stage.at[t], out.at[s, tm], out_send.at[t], out_recv.at[s, tm], tm=there).start()

        for d in FAR:
            wait(sbuf.at[slot, d], ex_send.at[slot, d])
        return carry

    lax.fori_loop(1, STEPS, step, 0)

    def drain(t, carry):
        @pl.when(forwards(t))
        def _():
            wait(ja.at[t, pl.ds(0, 3)], xsend.at[t, 0])
            wait(ia.at[t, pl.ds(0, 3 * Q)], xsend.at[t, 1])

        @pl.when(lax.rem(t // 2, 2) == core)
        def _():
            wait(ja.at[t], sibsend.at[t, 0])
            wait(ia.at[t], sibsend.at[t, 1])

        @pl.when(t // 2 != tm)
        def _():
            wait(stage.at[t], out_send.at[t])

        return carry

    lax.fori_loop(1, STEPS, drain, 0)
    for s in range(2):
        @pl.when(jnp.logical_or(tm != 0, s == 1))
        def _(s=s):
            wait(ja.at[0, pl.ds(0, 3)], ysend.at[s, 0])
            wait(ia.at[0, pl.ds(0, 3 * Q)], ysend.at[s, 1])
            for g in range(TM):
                wait(stage.at[0], out_recv.at[s, g])

    for d in range(1, TM):
        wait(gain.at[0], gain_send.at[d])

    @pl.when(tm == 0)
    def _():
        pltpu.make_async_copy(wide_out, out.at[0], out_recv.at[0, 0]).wait()
        for g in range(1, TM):
            wait(state, first_send.at[g])


def local(jac, block_cols, iface_jac, iface_send, iface_recv, iface_live, ctrl_node, ctrl_gain):
    node = jnp.broadcast_to(ctrl_node.reshape(TM, W, 1), (TM, W, BLK))
    gain = jnp.broadcast_to(
        ctrl_gain.reshape(2, TM, W, 1).transpose(1, 0, 2, 3), (TM, 2, W, BLK)
    )
    smem = pl.BlockSpec(memory_space=pltpu.SMEM)
    vmem = pl.BlockSpec(memory_space=pltpu.VMEM)
    hbm = pl.BlockSpec(memory_space=pl.ANY)
    dma = pltpu.SemaphoreType.DMA
    bf16, f32 = jnp.bfloat16, jnp.float32
    out = pl.pallas_call(
        kernel,
        out_shape=jax.ShapeDtypeStruct((2, TM, W, NB * BLK), bf16),
        in_specs=[hbm, hbm, smem, smem, smem, smem, vmem, vmem],
        out_specs=hbm,
        scratch_shapes=[
            pltpu.VMEM((STEPS, NB, 3, BLK, BLK), bf16),
            pltpu.VMEM((STEPS, NET, BLK, BLK), bf16),
            pltpu.VMEM((STEPS, W, BLK), f32),
            pltpu.VMEM((NB, W, BLK), bf16),
            pltpu.VMEM((NB, WIDE, BLK), bf16),
            pltpu.VMEM((TM, NB, W, BLK), bf16),
            pltpu.VMEM((TM, W, NB * BLK), bf16),
            pltpu.VMEM((STEPS, W, NB * BLK), bf16),
            pltpu.VMEM((2, NET, W, BLK), bf16),
            pltpu.VMEM((2, NET, W, BLK), bf16),
            dma((2, 2)),
            dma((STEPS, COLS, 2)),
            dma((STEPS, 2)),
            dma((2, 2)),
            dma((STEPS, 2)),
            dma((STEPS, 2)),
            dma((TM,)),
            dma((TM,)),
            dma((TM,)),
            dma,
            dma((2, NET)),
            dma((2, NET)),
            dma((STEPS,)),
            dma((2, TM)),
        ],
        compiler_params=pltpu.CompilerParams(
            collective_id=0, has_side_effects=True, vmem_limit_bytes=40 << 20
        ),
    )(
        jac, iface_jac.reshape(2, NET, BLK, BLK),
        block_cols, iface_send, iface_recv, iface_live, node, gain,
    )
    return out.reshape(2, WIDE, NB * BLK)


def solution(mesh):
    return jax.shard_map(
        local,
        mesh=mesh,
        in_specs=(
            P("tm", "net", None, None, None),
            P("net", None),
            P("tm", "net", None, None, None),
            P("net", None),
            P("net", None),
            P("net", None),
            P("cols"),
            P("tm", "cols"),
        ),
        out_specs=P("tm", "cols", "net"),
        check_vma=False,
    )
```

```python
import jax
import jax.numpy as jnp
from jax import lax
from jax.experimental import pallas as pl
from jax.experimental.pallas import tpu as pltpu
from jax.sharding import PartitionSpec as P

MESH = pl.DeviceIdType.MESH
TM = 8
NET = 16
COLS = 4
NB = 4
BLK = 128
STEPS = 16
WIDE = 192
W = WIDE // TM
Q = NET // COLS
NEAR = sorted(range(1, NET), key=lambda d: min(d, NET - d))
FAR = NEAR[::-1]
GROUPS = (NEAR[:8], NEAR[8:])


def dot_t(x, w):
    return lax.dot_general(
        x, w, (((1,), (1,)), ((), ())), preferred_element_type=jnp.float32
    )


def kernel(
    jac, iface, bcols_hbm, send_hbm, recv_hbm, live_hbm, node_hbm, gain_hbm, out,
    ja, ia, bcols, send, recv, live, node_row, gains, state, zero, wide, wide_out, stage, sbuf, rbuf,
    small_sem, own_sem, quarter_sem, sib_sem, ysend, sibsend, xsend,
    gain_send, gain_recv, first_send, first_recv,
    ex_send, ex_recv, out_send, out_recv,
):
    tm = lax.axis_index("tm")
    me = lax.axis_index("net")
    x = lax.axis_index("cols")
    y, core = tm // 2, lax.rem(tm, 2)
    sibling = 2 * y + 1 - core
    lane = lax.broadcasted_iota(jnp.int32, (1, BLK), 1)

    def remote(src, dst, ssem, rsem, **device):
        return pltpu.make_async_remote_copy(
            src_ref=src, dst_ref=dst, send_sem=ssem, recv_sem=rsem,
            device_id=device, device_id_type=MESH,
        )

    def wait(ref, sem):
        pltpu.make_async_copy(ref, ref, sem).wait()

    barrier = pltpu.get_barrier_semaphore()
    for d in FAR:
        pl.semaphore_signal(barrier, inc=1, device_id={"net": lax.rem(me + d, NET)}, device_id_type=MESH)
    for d in range(1, TM):
        pl.semaphore_signal(barrier, inc=1, device_id={"tm": lax.rem(tm + d, TM)}, device_id_type=MESH)
    for d in range(1, COLS):
        pl.semaphore_signal(barrier, inc=1, device_id={"cols": lax.rem(x + d, COLS)}, device_id_type=MESH)

    own = [
        pltpu.make_async_copy(src, dst, small_sem.at[n])
        for n, (src, dst) in enumerate((
            (bcols_hbm, bcols), (send_hbm, send), (recv_hbm, recv), (live_hbm, live),
            (node_hbm, node_row), (gain_hbm, gains.at[tm]),
        ))
    ]
    for s in range(2):
        own.append(pltpu.make_async_copy(jac.at[s], ja.at[2 * tm + s], own_sem.at[s, 0]))
        own.append(pltpu.make_async_copy(iface.at[s, 0], ia.at[2 * tm + s], own_sem.at[s, 1]))
    for copy in own:
        copy.start()

    def near_terms(t, ref):
        sums = []
        for i in range(NB):
            values = jnp.concatenate([ref[i], ref[bcols[0, i]], ref[bcols[1, i]]], axis=1)
            weights = jnp.concatenate([ja[t, i, 0], ja[t, i, 1], ja[t, i, 2]], axis=1)
            sums.append(dot_t(values, weights))
        return sums

    def add_interface(sums, t, q, values):
        term = dot_t(values, ia[t, q])
        reach, block = live[0, q], recv[0, q]
        return [
            total + jnp.where(lane < jnp.where(block == i, reach, 0), term, 0.0)
            for i, total in enumerate(sums)
        ]

    wide_lane = lax.broadcasted_iota(jnp.int32, (W, WIDE), 1)
    wide_row = lax.broadcasted_iota(jnp.int32, (W, WIDE), 0)

    def column(row, g):
        picked = jnp.where(wide_lane == wide_row + g * W, row, jnp.zeros_like(row))
        return jnp.broadcast_to(jnp.sum(picked, axis=1, keepdims=True), (W, BLK))

    def nodes_of(g):
        return column(node_row[...].reshape(1, WIDE).astype(jnp.float32), g).astype(jnp.int32)

    def inject(total, i, nodes, gain_rows):
        return total + jnp.where(nodes == lane + (me * NB + i) * BLK, gain_rows, 0.0)

    for copy in own:
        copy.wait()

    @pl.when(tm == 0)
    def _():
        zero[...] = jnp.zeros_like(zero)
        sums = near_terms(0, zero)
        for q in range(NET):
            sums = add_interface(sums, 0, q, zero[0])
        for g in range(TM):
            nodes, gain_rows = nodes_of(g), column(gains[0, 0:1], g)
            for i in range(NB):
                new = inject(sums[i], i, nodes, gain_rows).astype(jnp.bfloat16)
                wide[g, i] = new
                wide_out[g, :, i * BLK : (i + 1) * BLK] = new
        pltpu.make_async_copy(wide_out, out.at[0], out_recv.at[0, 0]).start()
        state[...] = wide[0]

    pl.semaphore_wait(barrier, NET - 1 + TM - 1 + COLS - 1)

    @pl.when(tm == 0)
    def _():
        for g in range(1, TM):
            remote(wide.at[g], state, first_send.at[g], first_recv, tm=g).start()

    def j_part(t, k):
        return ja.at[t, k]

    def i_part(t, k):
        return ia.at[t, pl.ds(k * Q, Q)]

    def spread_own(t):
        s = lax.rem(t, 2)
        for d in range(1, 4):
            there = 2 * lax.rem(y + d, 4) + core
            remote(jac.at[s, x], j_part(t, x), ysend.at[s, 0], quarter_sem.at[t, x, 0], tm=there).start()
            remote(iface.at[s, 0, pl.ds(x * Q, Q)], i_part(t, x), ysend.at[s, 1], quarter_sem.at[t, x, 1], tm=there).start()
        remote(jac.at[s], ja.at[t], sibsend.at[t, 0], sib_sem.at[t, 0], tm=sibling).start()
        remote(iface.at[s, 0], ia.at[t], sibsend.at[t, 1], sib_sem.at[t, 1], tm=sibling).start()

    def to_sibling(t, k):
        remote(j_part(t, k), j_part(t, k), sibsend.at[t, 0], sib_sem.at[t, 0], tm=sibling).start()
        remote(i_part(t, k), i_part(t, k), sibsend.at[t, 1], sib_sem.at[t, 1], tm=sibling).start()

    def forwards(t):
        return jnp.logical_and(
            t < STEPS, jnp.logical_and(lax.rem(t // 2, 2) == core, t // 4 != y)
        )

    def forward_own_quarter(t):
        @pl.when(forwards(t))
        def _():
            wait(j_part(t, x), quarter_sem.at[t, x, 0])
            wait(i_part(t, x), quarter_sem.at[t, x, 1])
            for d in range(1, COLS):
                there = lax.rem(x + d, COLS)
                remote(j_part(t, x), j_part(t, x), xsend.at[t, 0], quarter_sem.at[t, x, 0], cols=there).start()
                remote(i_part(t, x), i_part(t, x), xsend.at[t, 1], quarter_sem.at[t, x, 1], cols=there).start()
            to_sibling(t, x)

    def forward_other_quarters(t):
        @pl.when(forwards(t))
        def _():
            for d in range(1, COLS):
                k = lax.rem(x + d, COLS)
                wait(j_part(t, k), quarter_sem.at[t, k, 0])
                wait(i_part(t, k), quarter_sem.at[t, k, 1])
                to_sibling(t, k)

    def from_sibling(t):
        @pl.when(lax.rem(t // 2, 2) != core)
        def _():
            wait(ja.at[t], sib_sem.at[t, 0])
            wait(ia.at[t], sib_sem.at[t, 1])

    def spread(t):
        @pl.when(jnp.logical_and(t < STEPS, t // 2 == tm))
        def _():
            spread_own(t)

    spread(1)

    for d in range(1, TM):
        there = lax.rem(tm + d, TM)
        remote(gain_hbm, gains.at[tm], gain_send.at[d], gain_recv.at[d], tm=there).start()

    @pl.when(tm != 0)
    def _():
        wait(state, first_recv)

    spread(2)
    spread(3)

    def exchange(t):
        slot = lax.rem(t, 2)
        for d in FAR:
            p = lax.rem(me + d, NET)
            sbuf[slot, d] = state[send[0, p]]
            remote(sbuf.at[slot, d], rbuf.at[slot, d], ex_send.at[slot, d], ex_recv.at[slot, d], net=p).start()

    def output(t):
        there, s = t // 2, lax.rem(t, 2)

        @pl.when(there == tm)
        def _():
            pltpu.make_async_copy(stage.at[t], out.at[s, tm], out_recv.at[s, tm]).start()

        @pl.when(there != tm)
        def _():
            remote(stage.at[t], out.at[s, tm], out_send.at[t], out_recv.at[s, tm], tm=there).start()

    def sent(slot):
        for d in FAR:
            wait(sbuf.at[slot, d], ex_send.at[slot, d])

    nodes = nodes_of(tm)

    def step(t, carry):
        slot = lax.rem(t, 2)
        exchange(t)

        @pl.when(t > 1)
        def _():
            output(t - 1)
            sent(1 - slot)

        spread(t + 3)

        @pl.when(t == 1)
        def _():
            forward_own_quarter(1)
            forward_other_quarters(1)
            forward_own_quarter(2)
            for d in range(1, TM):
                wait(gains.at[lax.rem(tm - d + TM, TM)], gain_recv.at[d])

        @pl.when(t == 2)
        def _():
            forward_other_quarters(2)
            forward_own_quarter(3)

        @pl.when(t == 3)
        def _():
            forward_other_quarters(3)

        @pl.when(t >= 2)
        def _():
            forward_own_quarter(t + 2)

        @pl.when(t >= 3)
        def _():
            forward_other_quarters(t + 1)

        from_sibling(t)

        gain_rows = column(gains[t // 2, pl.ds(lax.rem(t, 2), 1)], tm)
        sums = [inject(total, i, nodes, gain_rows) for i, total in enumerate(near_terms(t, state))]
        sums = add_interface(sums, t, me, state[send[0, me]])
        for group in GROUPS:
            for d in group:
                wait(rbuf.at[slot, d], ex_recv.at[slot, d])
            for d in group:
                sums = add_interface(sums, t, lax.rem(me - d + NET, NET), rbuf[slot, d])
        for i in range(NB):
            new = sums[i].astype(jnp.bfloat16)
            state[i] = new
            stage[t, :, i * BLK : (i + 1) * BLK] = new
        return carry

    lax.fori_loop(1, STEPS, step, 0)
    output(STEPS - 1)
    sent((STEPS - 1) % 2)

    def drain(t, carry):
        @pl.when(forwards(t))
        def _():
            wait(ja.at[t, pl.ds(0, 3)], xsend.at[t, 0])
            wait(ia.at[t, pl.ds(0, 3 * Q)], xsend.at[t, 1])

        @pl.when(lax.rem(t // 2, 2) == core)
        def _():
            wait(ja.at[t], sibsend.at[t, 0])
            wait(ia.at[t], sibsend.at[t, 1])

        @pl.when(t // 2 != tm)
        def _():
            wait(stage.at[t], out_send.at[t])

        return carry

    lax.fori_loop(1, STEPS, drain, 0)
    for s in range(2):
        @pl.when(jnp.logical_or(tm != 0, s == 1))
        def _(s=s):
            wait(ja.at[0, pl.ds(0, 3)], ysend.at[s, 0])
            wait(ia.at[0, pl.ds(0, 3 * Q)], ysend.at[s, 1])
            for g in range(TM):
                wait(stage.at[0], out_recv.at[s, g])

    for d in range(1, TM):
        wait(gains.at[0], gain_send.at[d])

    @pl.when(tm == 0)
    def _():
        pltpu.make_async_copy(wide_out, out.at[0], out_recv.at[0, 0]).wait()
        for g in range(1, TM):
            wait(state, first_send.at[g])


def local(jac, block_cols, iface_jac, iface_send, iface_recv, iface_live, ctrl_node, ctrl_gain):
    hbm = pl.BlockSpec(memory_space=pltpu.HBM)
    dma = pltpu.SemaphoreType.DMA
    bf16, f32, i32 = jnp.bfloat16, jnp.float32, jnp.int32
    out = pl.pallas_call(
        kernel,
        out_shape=jax.ShapeDtypeStruct((2, TM, W, NB * BLK), bf16),
        in_specs=[hbm] * 8,
        out_specs=hbm,
        scratch_shapes=[
            pltpu.VMEM((STEPS, NB, 3, BLK, BLK), bf16),
            pltpu.VMEM((STEPS, NET, BLK, BLK), bf16),
            pltpu.SMEM((2, NB), i32),
            pltpu.SMEM((1, NET), i32),
            pltpu.SMEM((1, NET), i32),
            pltpu.SMEM((1, NET), i32),
            pltpu.VMEM((WIDE,), i32),
            pltpu.VMEM((TM, 2, WIDE), f32),
            pltpu.VMEM((NB, W, BLK), bf16),
            pltpu.VMEM((NB, W, BLK), bf16),
            pltpu.VMEM((TM, NB, W, BLK), bf16),
            pltpu.VMEM((TM, W, NB * BLK), bf16),
            pltpu.VMEM((STEPS, W, NB * BLK), bf16),
            pltpu.VMEM((2, NET, W, BLK), bf16),
            pltpu.VMEM((2, NET, W, BLK), bf16),
            dma((6,)),
            dma((2, 2)),
            dma((STEPS, COLS, 2)),
            dma((STEPS, 2)),
            dma((2, 2)),
            dma((STEPS, 2)),
            dma((STEPS, 2)),
            dma((TM,)),
            dma((TM,)),
            dma((TM,)),
            dma,
            dma((2, NET)),
            dma((2, NET)),
            dma((STEPS,)),
            dma((2, TM)),
        ],
        compiler_params=pltpu.CompilerParams(
            collective_id=0, has_side_effects=True, vmem_limit_bytes=60 << 20
        ),
    )(
        jac, iface_jac, block_cols.T, iface_send, iface_recv, iface_live, ctrl_node, ctrl_gain
    )
    return out.reshape(2, WIDE, NB * BLK)


def solution(mesh):
    return jax.shard_map(
        local,
        mesh=mesh,
        in_specs=(
            P("tm", "net", None, None, None),
            P("net", None),
            P("tm", "net", None, None, None),
            P("net", None),
            P("net", None),
            P("net", None),
            P("cols"),
            P("tm", "cols"),
        ),
        out_specs=P("tm", "cols", "net"),
        check_vma=False,
    )
```

```python
import jax
import jax.numpy as jnp
from jax import lax
from jax.experimental import pallas as pl
from jax.experimental.pallas import tpu as pltpu
from jax.sharding import PartitionSpec as P

MESH = pl.DeviceIdType.MESH
TM = 8
NET = 16
COLS = 4
NB = 4
BLK = 128
STEPS = 16
WIDE = 192
W = WIDE // TM
Q = NET // COLS
NEAR = sorted(range(1, NET), key=lambda d: min(d, NET - d))
FAR = NEAR[::-1]
GROUPS = (NEAR[:8], NEAR[8:])


def dot_t(x, w):
    return lax.dot_general(
        x, w, (((1,), (1,)), ((), ())), preferred_element_type=jnp.float32
    )


def kernel(
    jac, iface, bcols_hbm, send_hbm, recv_hbm, live_hbm, node_hbm, gain_hbm, out,
    ja, ia, bcols, send, recv, live, node_row, gains, state, zero, wide, wide_out, stage, sbuf, rbuf,
    small_sem, own_sem, quarter_sem, sib_sem, ysend, sibsend, xsend,
    gain_send, gain_recv, first_send, first_recv,
    ex_send, ex_recv, out_send, out_recv,
):
    tm = lax.axis_index("tm")
    me = lax.axis_index("net")
    x = lax.axis_index("cols")
    y, core = tm // 2, lax.rem(tm, 2)
    sibling = 2 * y + 1 - core
    lane = lax.broadcasted_iota(jnp.int32, (1, BLK), 1)

    def remote(src, dst, ssem, rsem, **device):
        return pltpu.make_async_remote_copy(
            src_ref=src, dst_ref=dst, send_sem=ssem, recv_sem=rsem,
            device_id=device, device_id_type=MESH,
        )

    def wait(ref, sem):
        pltpu.make_async_copy(ref, ref, sem).wait()

    barrier = pltpu.get_barrier_semaphore()
    for d in FAR:
        pl.semaphore_signal(barrier, inc=1, device_id={"net": lax.rem(me + d, NET)}, device_id_type=MESH)
    for d in range(1, TM):
        pl.semaphore_signal(barrier, inc=1, device_id={"tm": lax.rem(tm + d, TM)}, device_id_type=MESH)
    for d in range(1, COLS):
        pl.semaphore_signal(barrier, inc=1, device_id={"cols": lax.rem(x + d, COLS)}, device_id_type=MESH)

    own = [
        pltpu.make_async_copy(src, dst, small_sem.at[n])
        for n, (src, dst) in enumerate((
            (bcols_hbm, bcols), (send_hbm, send), (recv_hbm, recv), (live_hbm, live),
            (node_hbm, node_row), (gain_hbm, gains.at[tm]),
        ))
    ]
    for s in range(2):
        own.append(pltpu.make_async_copy(jac.at[s], ja.at[2 * tm + s], own_sem.at[s, 0]))
        own.append(pltpu.make_async_copy(iface.at[s, 0], ia.at[2 * tm + s], own_sem.at[s, 1]))
    for copy in own:
        copy.start()

    def near_terms(t, ref):
        sums = []
        for i in range(NB):
            values = jnp.concatenate([ref[i], ref[bcols[0, i]], ref[bcols[1, i]]], axis=1)
            weights = jnp.concatenate([ja[t, i, 0], ja[t, i, 1], ja[t, i, 2]], axis=1)
            sums.append(dot_t(values, weights))
        return sums

    def add_interface(sums, t, q, values):
        term = dot_t(values, ia[t, q])
        reach, block = live[0, q], recv[0, q]
        return [
            total + jnp.where(lane < jnp.where(block == i, reach, 0), term, 0.0)
            for i, total in enumerate(sums)
        ]

    wide_lane = lax.broadcasted_iota(jnp.int32, (W, WIDE), 1)
    wide_row = lax.broadcasted_iota(jnp.int32, (W, WIDE), 0)

    def column(row, g):
        picked = jnp.where(wide_lane == wide_row + g * W, row, jnp.zeros_like(row))
        return jnp.broadcast_to(jnp.sum(picked, axis=1, keepdims=True), (W, BLK))

    def nodes_of(g):
        return column(node_row[...].reshape(1, WIDE).astype(jnp.float32), g).astype(jnp.int32)

    def inject(total, i, nodes, gain_rows):
        return total + jnp.where(nodes == lane + (me * NB + i) * BLK, gain_rows, 0.0)

    for copy in own:
        copy.wait()

    @pl.when(tm == 0)
    def _():
        zero[...] = jnp.zeros_like(zero)
        sums = near_terms(0, zero)
        for q in range(NET):
            sums = add_interface(sums, 0, q, zero[0])
        for g in range(TM):
            nodes, gain_rows = nodes_of(g), column(gains[0, 0:1], g)
            for i in range(NB):
                new = inject(sums[i], i, nodes, gain_rows).astype(jnp.bfloat16)
                wide[g, i] = new
                wide_out[g, :, i * BLK : (i + 1) * BLK] = new
        pltpu.make_async_copy(wide_out, out.at[0], out_recv.at[0, 0]).start()
        state[...] = wide[0]

    pl.semaphore_wait(barrier, NET - 1 + TM - 1 + COLS - 1)

    @pl.when(tm == 0)
    def _():
        for g in range(1, TM):
            remote(wide.at[g], state, first_send.at[g], first_recv, tm=g).start()

    def part(t, k, kind):
        return ja.at[t, k] if kind == 0 else ia.at[t, pl.ds(k * Q, Q)]

    def whole(t, kind):
        return ja.at[t] if kind == 0 else ia.at[t]

    def three_parts(kind):
        return ja.at[0, pl.ds(0, 3)] if kind == 0 else ia.at[0, pl.ds(0, 3 * Q)]

    def spread_own(t):
        s = lax.rem(t, 2)
        for d in (1, 3, 2):
            row = lax.rem(y + d, 4)
            remote(jac.at[s, x], part(t, x, 0), ysend.at[s, 0], quarter_sem.at[t, x], tm=2 * row).start()
            remote(iface.at[s, 0, pl.ds(x * Q, Q)], part(t, x, 1), ysend.at[s, 1], quarter_sem.at[t, x], tm=2 * row + 1).start()
        remote(jac.at[s], ja.at[t], sibsend.at[t, 0], sib_sem.at[t, 0], tm=sibling).start()
        remote(iface.at[s, 0], ia.at[t], sibsend.at[t, 1], sib_sem.at[t, 1], tm=sibling).start()

    def forwarding(t, act):
        for kind in range(2):
            @pl.when(jnp.logical_and(jnp.logical_and(t < STEPS, t // 4 != y), core == kind))
            def _(kind=kind):
                act(kind)

    def to_sibling(t, k, kind):
        remote(part(t, k, kind), part(t, k, kind), sibsend.at[t, kind], sib_sem.at[t, kind], tm=sibling).start()

    def forward_own_quarter(t):
        def act(kind):
            wait(part(t, x, kind), quarter_sem.at[t, x])
            for d in (1, 3, 2):
                remote(part(t, x, kind), part(t, x, kind), xsend.at[t], quarter_sem.at[t, x], cols=lax.rem(x + d, COLS)).start()
            to_sibling(t, x, kind)

        forwarding(t, act)

    def forward_other_quarters(t):
        def act(kind):
            for d in (1, 3, 2):
                k = lax.rem(x + d, COLS)
                wait(part(t, k, kind), quarter_sem.at[t, k])
                to_sibling(t, k, kind)

        forwarding(t, act)

    def from_sibling(t):
        for kind in range(2):
            here = jnp.logical_and(t // 4 != y, core != kind)
            here = jnp.logical_or(here, jnp.logical_and(t // 4 == y, t // 2 != tm))

            @pl.when(here)
            def _(kind=kind):
                wait(whole(t, kind), sib_sem.at[t, kind])

    def spread(t):
        @pl.when(jnp.logical_and(t < STEPS, t // 2 == tm))
        def _():
            spread_own(t)

    spread(1)

    for d in range(1, TM):
        there = lax.rem(tm + d, TM)
        remote(gain_hbm, gains.at[tm], gain_send.at[d], gain_recv.at[d], tm=there).start()

    @pl.when(tm != 0)
    def _():
        wait(state, first_recv)

    def exchange(t):
        slot = lax.rem(t, 2)
        for d in FAR:
            p = lax.rem(me + d, NET)
            sbuf[slot, d] = state[send[0, p]]
            remote(sbuf.at[slot, d], rbuf.at[slot, d], ex_send.at[slot, d], ex_recv.at[slot, d], net=p).start()

    def output(t):
        there, s = t // 2, lax.rem(t, 2)

        @pl.when(there == tm)
        def _():
            pltpu.make_async_copy(stage.at[t], out.at[s, tm], out_recv.at[s, tm]).start()

        @pl.when(there != tm)
        def _():
            remote(stage.at[t], out.at[s, tm], out_send.at[t], out_recv.at[s, tm], tm=there).start()

    def sent(slot):
        for d in FAR:
            wait(sbuf.at[slot, d], ex_send.at[slot, d])

    nodes = nodes_of(tm)

    def step(t, carry):
        slot = lax.rem(t, 2)
        exchange(t)

        @pl.when(t > 1)
        def _():
            output(t - 1)
            sent(1 - slot)

        @pl.when(t == 1)
        def _():
            spread(2)
            forward_own_quarter(1)
            forward_other_quarters(1)
            forward_own_quarter(2)
            for d in range(1, TM):
                wait(gains.at[lax.rem(tm - d + TM, TM)], gain_recv.at[d])

        @pl.when(t == 2)
        def _():
            forward_other_quarters(2)
            forward_own_quarter(3)

        @pl.when(t == 3)
        def _():
            forward_other_quarters(3)

        @pl.when(t >= 2)
        def _():
            spread(t + 3)
            forward_own_quarter(t + 2)

        @pl.when(t >= 3)
        def _():
            forward_other_quarters(t + 1)

        from_sibling(t)

        @pl.when(t == 1)
        def _():
            spread(3)
            spread(4)

        gain_rows = column(gains[t // 2, pl.ds(lax.rem(t, 2), 1)], tm)
        sums = [inject(total, i, nodes, gain_rows) for i, total in enumerate(near_terms(t, state))]
        sums = add_interface(sums, t, me, state[send[0, me]])
        for group in GROUPS:
            for d in group:
                wait(rbuf.at[slot, d], ex_recv.at[slot, d])
            for d in group:
                sums = add_interface(sums, t, lax.rem(me - d + NET, NET), rbuf[slot, d])
        for i in range(NB):
            new = sums[i].astype(jnp.bfloat16)
            state[i] = new
            stage[t, :, i * BLK : (i + 1) * BLK] = new
        return carry

    lax.fori_loop(1, STEPS, step, 0)
    output(STEPS - 1)
    sent((STEPS - 1) % 2)

    def drain(t, carry):
        def act(kind):
            wait(three_parts(kind), xsend.at[t])
            wait(whole(t, kind), sibsend.at[t, kind])

        forwarding(t, act)

        @pl.when(t // 2 == tm)
        def _():
            for kind in range(2):
                wait(three_parts(kind), ysend.at[lax.rem(t, 2), kind])
                wait(whole(t, kind), sibsend.at[t, kind])

        @pl.when(t // 2 != tm)
        def _():
            wait(stage.at[t], out_send.at[t])

        return carry

    lax.fori_loop(1, STEPS, drain, 0)
    for s in range(2):
        @pl.when(jnp.logical_or(tm != 0, s == 1))
        def _(s=s):
            for g in range(TM):
                wait(stage.at[0], out_recv.at[s, g])

    for d in range(1, TM):
        wait(gains.at[0], gain_send.at[d])

    @pl.when(tm == 0)
    def _():
        pltpu.make_async_copy(wide_out, out.at[0], out_recv.at[0, 0]).wait()
        for g in range(1, TM):
            wait(state, first_send.at[g])


def local(jac, block_cols, iface_jac, iface_send, iface_recv, iface_live, ctrl_node, ctrl_gain):
    hbm = pl.BlockSpec(memory_space=pltpu.HBM)
    dma = pltpu.SemaphoreType.DMA
    bf16, f32, i32 = jnp.bfloat16, jnp.float32, jnp.int32
    out = pl.pallas_call(
        kernel,
        out_shape=jax.ShapeDtypeStruct((2, TM, W, NB * BLK), bf16),
        in_specs=[hbm] * 8,
        out_specs=hbm,
        scratch_shapes=[
            pltpu.VMEM((STEPS, NB, 3, BLK, BLK), bf16),
            pltpu.VMEM((STEPS, NET, BLK, BLK), bf16),
            pltpu.SMEM((2, NB), i32),
            pltpu.SMEM((1, NET), i32),
            pltpu.SMEM((1, NET), i32),
            pltpu.SMEM((1, NET), i32),
            pltpu.VMEM((WIDE,), i32),
            pltpu.VMEM((TM, 2, WIDE), f32),
            pltpu.VMEM((NB, W, BLK), bf16),
            pltpu.VMEM((NB, W, BLK), bf16),
            pltpu.VMEM((TM, NB, W, BLK), bf16),
            pltpu.VMEM((TM, W, NB * BLK), bf16),
            pltpu.VMEM((STEPS, W, NB * BLK), bf16),
            pltpu.VMEM((2, NET, W, BLK), bf16),
            pltpu.VMEM((2, NET, W, BLK), bf16),
            dma((6,)),
            dma((2, 2)),
            dma((STEPS, COLS)),
            dma((STEPS, 2)),
            dma((2, 2)),
            dma((STEPS, 2)),
            dma((STEPS,)),
            dma((TM,)),
            dma((TM,)),
            dma((TM,)),
            dma,
            dma((2, NET)),
            dma((2, NET)),
            dma((STEPS,)),
            dma((2, TM)),
        ],
        compiler_params=pltpu.CompilerParams(
            collective_id=0, has_side_effects=True, vmem_limit_bytes=60 << 20
        ),
    )(
        jac, iface_jac, block_cols.T, iface_send, iface_recv, iface_live, ctrl_node, ctrl_gain
    )
    return out.reshape(2, WIDE, NB * BLK)


def solution(mesh):
    return jax.shard_map(
        local,
        mesh=mesh,
        in_specs=(
            P("tm", "net", None, None, None),
            P("net", None),
            P("tm", "net", None, None, None),
            P("net", None),
            P("net", None),
            P("net", None),
            P("cols"),
            P("tm", "cols"),
        ),
        out_specs=P("tm", "cols", "net"),
        check_vma=False,
    )
```

```python
import jax
import jax.numpy as jnp
from jax import lax
from jax.experimental import pallas as pl
from jax.experimental.pallas import tpu as pltpu
from jax.sharding import PartitionSpec as P

MESH = pl.DeviceIdType.MESH
TM = 8
NET = 16
COLS = 4
NB = 4
BLK = 128
STEPS = 16
WIDE = 192
W = WIDE // TM
Q = NET // COLS
NEAR = sorted(range(1, NET), key=lambda d: min(d, NET - d))
FAR = NEAR[::-1]
GROUPS = (NEAR[:8], NEAR[8:])


def dot_t(x, w):
    return lax.dot_general(
        x, w, (((1,), (1,)), ((), ())), preferred_element_type=jnp.float32
    )


def kernel(
    jac, iface, bcols_hbm, send_hbm, recv_hbm, live_hbm, node_hbm, gain_hbm, out,
    ja, ia, bcols, send, recv, live, node_row, gains, meta, state, zero, wide, wide_out, node_cols, gain_cols, first, acc, stage, sbuf, rbuf,
    small_sem, own_sem, quarter_sem, sib_sem, ysend, sibsend, xsend,
    gain_send, gain_recv, meta_send, meta_recv, first_send, first_recv,
    ex_send, ex_recv, out_send, out_recv,
):
    tm = lax.axis_index("tm")
    me = lax.axis_index("net")
    x = lax.axis_index("cols")
    y, core = tm // 2, lax.rem(tm, 2)
    sibling = 2 * y + 1 - core
    lane = lax.broadcasted_iota(jnp.int32, (1, BLK), 1)

    def remote(src, dst, ssem, rsem, **device):
        return pltpu.make_async_remote_copy(
            src_ref=src, dst_ref=dst, send_sem=ssem, recv_sem=rsem,
            device_id=device, device_id_type=MESH,
        )

    def wait(ref, sem):
        pltpu.make_async_copy(ref, ref, sem).wait()

    barrier = pltpu.get_barrier_semaphore()
    for d in FAR:
        pl.semaphore_signal(barrier, inc=1, device_id={"net": lax.rem(me + d, NET)}, device_id_type=MESH)
    for d in range(1, TM):
        pl.semaphore_signal(barrier, inc=1, device_id={"tm": lax.rem(tm + d, TM)}, device_id_type=MESH)
    for d in range(1, COLS):
        pl.semaphore_signal(barrier, inc=1, device_id={"cols": lax.rem(x + d, COLS)}, device_id_type=MESH)

    own = [
        pltpu.make_async_copy(src, dst, small_sem.at[n])
        for n, (src, dst) in enumerate((
            (bcols_hbm, bcols), (send_hbm, send), (recv_hbm, recv), (live_hbm, live),
            (node_hbm, node_row), (gain_hbm, gains.at[tm]), (send_hbm, meta.at[me]),
        ))
    ]
    for s in range(2):
        own.append(pltpu.make_async_copy(jac.at[s], ja.at[2 * tm + s], own_sem.at[s, 0]))
        own.append(pltpu.make_async_copy(iface.at[s, 0], ia.at[2 * tm + s], own_sem.at[s, 1]))
    for copy in own:
        copy.start()

    def near_terms(t, ref):
        sums = []
        for i in range(NB):
            values = jnp.concatenate([ref[i], ref[bcols[0, i]], ref[bcols[1, i]]], axis=1)
            weights = jnp.concatenate([ja[t, i, 0], ja[t, i, 1], ja[t, i, 2]], axis=1)
            sums.append(dot_t(values, weights))
        return sums

    def add_interface(sums, t, q, values):
        term = dot_t(values, ia[t, q])
        reach, block = live[0, q], recv[0, q]
        return [
            total + jnp.where(lane < jnp.where(block == i, reach, 0), term, 0.0)
            for i, total in enumerate(sums)
        ]

    def column(row, start, rows):
        at = lax.broadcasted_iota(jnp.int32, (rows, WIDE), 1) == start + lax.broadcasted_iota(jnp.int32, (rows, WIDE), 0)
        picked = jnp.where(at, row, jnp.zeros_like(row))
        return jnp.broadcast_to(jnp.sum(picked, axis=1, keepdims=True), (rows, BLK))

    def nodes_of(start, rows):
        return column(node_row[...].reshape(1, WIDE).astype(jnp.float32), start, rows).astype(jnp.int32)

    def inject(total, i, nodes, gain_rows):
        return total + jnp.where(nodes == lane + (me * NB + i) * BLK, gain_rows, 0.0)

    for copy in own:
        copy.wait()

    def keep_wide(s, i, total):
        for g in range(TM):
            new = total[g * W : (g + 1) * W].astype(jnp.bfloat16)
            wide[g, i] = new
            wide_out[s, g, :, i * BLK : (i + 1) * BLK] = new

    @pl.when(tm == 0)
    def _():
        zero[...] = jnp.zeros_like(zero)
        sums = near_terms(0, zero)
        for q in range(NET):
            sums = add_interface(sums, 0, q, zero[0])
        node_cols[...] = nodes_of(0, WIDE)
        for s in range(2):
            gain_cols[s] = column(gains[0, s : s + 1], 0, WIDE)
        for i in range(NB):
            total = inject(jnp.concatenate([sums[i]] * TM, axis=0), i, node_cols[...], gain_cols[0])
            first[i] = total.astype(jnp.bfloat16)
            keep_wide(0, i, total)
        pltpu.make_async_copy(wide_out.at[0], out.at[0], out_recv.at[0, 0]).start()

    pl.semaphore_wait(barrier, NET - 1 + TM - 1 + COLS - 1)

    @pl.when(tm == 0)
    def _():
        for d in FAR:
            remote(send_hbm, meta.at[me], meta_send.at[d], meta_recv.at[d], net=lax.rem(me + d, NET)).start()

    def part(t, k, kind):
        return ja.at[t, k] if kind == 0 else ia.at[t, pl.ds(k * Q, Q)]

    def whole(t, kind):
        return ja.at[t] if kind == 0 else ia.at[t]

    def three_parts(kind):
        return ja.at[0, pl.ds(0, 3)] if kind == 0 else ia.at[0, pl.ds(0, 3 * Q)]

    def spread_own(t):
        s = lax.rem(t, 2)
        for d in (1, 3, 2):
            row = lax.rem(y + d, 4)
            remote(jac.at[s, x], part(t, x, 0), ysend.at[s, 0], quarter_sem.at[t, x], tm=2 * row).start()
            remote(iface.at[s, 0, pl.ds(x * Q, Q)], part(t, x, 1), ysend.at[s, 1], quarter_sem.at[t, x], tm=2 * row + 1).start()
        remote(jac.at[s], ja.at[t], sibsend.at[t, 0], sib_sem.at[t, 0], tm=sibling).start()
        remote(iface.at[s, 0], ia.at[t], sibsend.at[t, 1], sib_sem.at[t, 1], tm=sibling).start()

    def forwarding(t, act):
        for kind in range(2):
            @pl.when(jnp.logical_and(jnp.logical_and(t < STEPS, t // 4 != y), core == kind))
            def _(kind=kind):
                act(kind)

    def to_sibling(t, k, kind):
        remote(part(t, k, kind), part(t, k, kind), sibsend.at[t, kind], sib_sem.at[t, kind], tm=sibling).start()

    def forward_own_quarter(t):
        def act(kind):
            wait(part(t, x, kind), quarter_sem.at[t, x])
            for d in (1, 3, 2):
                remote(part(t, x, kind), part(t, x, kind), xsend.at[t], quarter_sem.at[t, x], cols=lax.rem(x + d, COLS)).start()
            to_sibling(t, x, kind)

        forwarding(t, act)

    def forward_other_quarters(t):
        def act(kind):
            for d in (1, 3, 2):
                k = lax.rem(x + d, COLS)
                wait(part(t, k, kind), quarter_sem.at[t, k])
                to_sibling(t, k, kind)

        forwarding(t, act)

    def from_sibling(t):
        for kind in range(2):
            here = jnp.logical_and(t // 4 != y, core != kind)
            here = jnp.logical_or(here, jnp.logical_and(t // 4 == y, t // 2 != tm))

            @pl.when(here)
            def _(kind=kind):
                wait(whole(t, kind), sib_sem.at[t, kind])

    def spread(t):
        @pl.when(jnp.logical_and(t < STEPS, t // 2 == tm))
        def _():
            spread_own(t)

    spread(2)

    for d in range(1, TM):
        there = lax.rem(tm + d, TM)
        remote(gain_hbm, gains.at[tm], gain_send.at[d], gain_recv.at[d], tm=there).start()

    @pl.when(tm == 0)
    def _():
        for i, total in enumerate(near_terms(1, first)):
            acc[i] = inject(total, i, node_cols[...], gain_cols[1])
        for d in FAR:
            wait(meta.at[0], meta_recv.at[d])

        def add(q, carry):
            mine = lax.broadcasted_iota(jnp.int32, (1, NET), 1) == me
            block = jnp.sum(jnp.where(mine, meta[q].astype(jnp.float32), 0.0), axis=1, keepdims=True)
            base = (q * NB + block.astype(jnp.int32)) * BLK
            values = jnp.where(node_cols[...] == lane + base, gain_cols[0], 0.0).astype(jnp.bfloat16)
            for i, total in enumerate(add_interface([acc[i] for i in range(NB)], 1, q, values)):
                acc[i] = total
            return carry

        lax.fori_loop(0, NET, add, 0)
        for i in range(NB):
            keep_wide(1, i, acc[i])
        for g in range(1, TM):
            remote(wide.at[g], state, first_send.at[g], first_recv, tm=g).start()
        state[...] = wide[0]
        pltpu.make_async_copy(wide_out.at[1], out.at[1], out_recv.at[1, 0]).start()

    def exchange(t):
        slot = lax.rem(t, 2)
        for d in FAR:
            p = lax.rem(me + d, NET)
            sbuf[slot, d] = state[send[0, p]]
            remote(sbuf.at[slot, d], rbuf.at[slot, d], ex_send.at[slot, d], ex_recv.at[slot, d], net=p).start()

    def output(t):
        there, s = t // 2, lax.rem(t, 2)

        @pl.when(there == tm)
        def _():
            pltpu.make_async_copy(stage.at[t], out.at[s, tm], out_recv.at[s, tm]).start()

        @pl.when(there != tm)
        def _():
            remote(stage.at[t], out.at[s, tm], out_send.at[t], out_recv.at[s, tm], tm=there).start()

    def sent(slot):
        for d in FAR:
            wait(sbuf.at[slot, d], ex_send.at[slot, d])

    nodes = nodes_of(tm * W, W)
    for d in range(1, TM):
        wait(gains.at[lax.rem(tm - d + TM, TM)], gain_recv.at[d])
    spread(3)
    forward_own_quarter(2)

    @pl.when(tm != 0)
    def _():
        wait(state, first_recv)


    def step(t, carry):
        slot = lax.rem(t, 2)
        exchange(t)

        @pl.when(t > 2)
        def _():
            output(t - 1)
            sent(1 - slot)

        forward_own_quarter(t + 1)
        forward_other_quarters(t)
        spread(t + 2)
        from_sibling(t)

        gain_rows = column(gains[t // 2, pl.ds(lax.rem(t, 2), 1)], tm * W, W)
        sums = [inject(total, i, nodes, gain_rows) for i, total in enumerate(near_terms(t, state))]
        sums = add_interface(sums, t, me, state[send[0, me]])
        for group in GROUPS:
            for d in group:
                wait(rbuf.at[slot, d], ex_recv.at[slot, d])
            for d in group:
                sums = add_interface(sums, t, lax.rem(me - d + NET, NET), rbuf[slot, d])
        for i in range(NB):
            new = sums[i].astype(jnp.bfloat16)
            state[i] = new
            stage[t, :, i * BLK : (i + 1) * BLK] = new
        return carry

    lax.fori_loop(2, STEPS, step, 0)
    output(STEPS - 1)
    sent((STEPS - 1) % 2)

    def drain(t, carry):
        def act(kind):
            wait(three_parts(kind), xsend.at[t])
            wait(whole(t, kind), sibsend.at[t, kind])

        forwarding(t, act)

        @pl.when(t // 2 == tm)
        def _():
            for kind in range(2):
                wait(three_parts(kind), ysend.at[lax.rem(t, 2), kind])
                wait(whole(t, kind), sibsend.at[t, kind])

        @pl.when(t // 2 != tm)
        def _():
            wait(stage.at[t], out_send.at[t])

        return carry

    lax.fori_loop(2, STEPS, drain, 0)
    @pl.when(tm != 0)
    def _():
        for s in range(2):
            for g in range(TM):
                wait(stage.at[0], out_recv.at[s, g])

    for d in range(1, TM):
        wait(gains.at[0], gain_send.at[d])

    @pl.when(tm == 0)
    def _():
        for s in range(2):
            pltpu.make_async_copy(wide_out.at[s], out.at[s], out_recv.at[s, 0]).wait()
        for g in range(1, TM):
            wait(state, first_send.at[g])
        for d in FAR:
            wait(meta.at[0], meta_send.at[d])


def local(jac, block_cols, iface_jac, iface_send, iface_recv, iface_live, ctrl_node, ctrl_gain):
    hbm = pl.BlockSpec(memory_space=pltpu.HBM)
    dma = pltpu.SemaphoreType.DMA
    bf16, f32, i32 = jnp.bfloat16, jnp.float32, jnp.int32
    out = pl.pallas_call(
        kernel,
        out_shape=jax.ShapeDtypeStruct((2, TM, W, NB * BLK), bf16),
        in_specs=[hbm] * 8,
        out_specs=hbm,
        scratch_shapes=[
            pltpu.VMEM((STEPS, NB, 3, BLK, BLK), bf16),
            pltpu.VMEM((STEPS, NET, BLK, BLK), bf16),
            pltpu.SMEM((2, NB), i32),
            pltpu.SMEM((1, NET), i32),
            pltpu.SMEM((1, NET), i32),
            pltpu.SMEM((1, NET), i32),
            pltpu.VMEM((WIDE,), i32),
            pltpu.VMEM((TM, 2, WIDE), f32),
            pltpu.VMEM((NET, 1, NET), i32),
            pltpu.VMEM((NB, W, BLK), bf16),
            pltpu.VMEM((NB, W, BLK), bf16),
            pltpu.VMEM((TM, NB, W, BLK), bf16),
            pltpu.VMEM((2, TM, W, NB * BLK), bf16),
            pltpu.VMEM((WIDE, BLK), i32),
            pltpu.VMEM((2, WIDE, BLK), f32),
            pltpu.VMEM((NB, WIDE, BLK), bf16),
            pltpu.VMEM((NB, WIDE, BLK), f32),
            pltpu.VMEM((STEPS, W, NB * BLK), bf16),
            pltpu.VMEM((2, NET, W, BLK), bf16),
            pltpu.VMEM((2, NET, W, BLK), bf16),
            dma((7,)),
            dma((2, 2)),
            dma((STEPS, COLS)),
            dma((STEPS, 2)),
            dma((2, 2)),
            dma((STEPS, 2)),
            dma((STEPS,)),
            dma((TM,)),
            dma((TM,)),
            dma((NET,)),
            dma((NET,)),
            dma((TM,)),
            dma,
            dma((2, NET)),
            dma((2, NET)),
            dma((STEPS,)),
            dma((2, TM)),
        ],
        compiler_params=pltpu.CompilerParams(
            collective_id=0, has_side_effects=True, vmem_limit_bytes=60 << 20
        ),
    )(
        jac, iface_jac, block_cols.T, iface_send, iface_recv, iface_live, ctrl_node, ctrl_gain
    )
    return out.reshape(2, WIDE, NB * BLK)


def solution(mesh):
    return jax.shard_map(
        local,
        mesh=mesh,
        in_specs=(
            P("tm", "net", None, None, None),
            P("net", None),
            P("tm", "net", None, None, None),
            P("net", None),
            P("net", None),
            P("net", None),
            P("cols"),
            P("tm", "cols"),
        ),
        out_specs=P("tm", "cols", "net"),
        check_vma=False,
    )
```

```python
import jax
import jax.numpy as jnp
from jax import lax
from jax.experimental import pallas as pl
from jax.experimental.pallas import tpu as pltpu
from jax.sharding import PartitionSpec as P

MESH = pl.DeviceIdType.MESH
TM = 8
NET = 16
COLS = 4
NB = 4
BLK = 128
STEPS = 16
WIDE = 192
W = WIDE // TM
Q = NET // COLS
NEAR = sorted(range(1, NET), key=lambda d: min(d, NET - d))
FAR = NEAR[::-1]
GROUPS = (NEAR[:10], NEAR[10:])


def dot_t(x, w):
    return lax.dot_general(
        x, w, (((1,), (1,)), ((), ())), preferred_element_type=jnp.float32
    )


def kernel(
    jac, iface, bcols_hbm, send_hbm, recv_hbm, live_hbm, node_hbm, gain_hbm, out,
    ja, ia, bcols, send, recv, live, node_row, gains, meta, state, pair, zero, wide, wide_out, node_cols, gain_cols, first, acc, stage, sbuf, rbuf,
    small_sem, own_sem, quarter_sem, sib_sem, ysend, sibsend, xsend,
    gain_send, gain_recv, meta_send, meta_recv, first_send, first_recv,
    ex_send, ex_recv, out_send, out_recv,
):
    tm = lax.axis_index("tm")
    me = lax.axis_index("net")
    x = lax.axis_index("cols")
    y, core = tm // 2, lax.rem(tm, 2)
    sibling = 2 * y + 1 - core
    lane = lax.broadcasted_iota(jnp.int32, (1, BLK), 1)

    def remote(src, dst, ssem, rsem, **device):
        return pltpu.make_async_remote_copy(
            src_ref=src, dst_ref=dst, send_sem=ssem, recv_sem=rsem,
            device_id=device, device_id_type=MESH,
        )

    def wait(ref, sem):
        pltpu.make_async_copy(ref, ref, sem).wait()

    barrier = pltpu.get_barrier_semaphore()
    for d in FAR:
        pl.semaphore_signal(barrier, inc=1, device_id={"net": lax.rem(me + d, NET)}, device_id_type=MESH)
    for d in range(1, TM):
        pl.semaphore_signal(barrier, inc=1, device_id={"tm": lax.rem(tm + d, TM)}, device_id_type=MESH)
    for d in range(1, COLS):
        pl.semaphore_signal(barrier, inc=1, device_id={"cols": lax.rem(x + d, COLS)}, device_id_type=MESH)

    own = [
        pltpu.make_async_copy(src, dst, small_sem.at[n])
        for n, (src, dst) in enumerate((
            (bcols_hbm, bcols), (send_hbm, send), (recv_hbm, recv), (live_hbm, live),
            (node_hbm, node_row), (gain_hbm, gains.at[tm]), (send_hbm, meta.at[me]),
        ))
    ]
    for s in range(2):
        own.append(pltpu.make_async_copy(jac.at[s], ja.at[2 * tm + s], own_sem.at[s, 0]))
        own.append(pltpu.make_async_copy(iface.at[s, 0], ia.at[2 * tm + s], own_sem.at[s, 1]))
    for copy in own:
        copy.start()

    def near_terms(t, ref):
        sums = []
        for i in range(NB):
            values = jnp.concatenate([ref[i], ref[bcols[0, i]], ref[bcols[1, i]]], axis=1)
            weights = jnp.concatenate([ja[t, i, 0], ja[t, i, 1], ja[t, i, 2]], axis=1)
            sums.append(dot_t(values, weights))
        return sums

    def add_interface(sums, t, q, values):
        term = dot_t(values, ia[t, q])
        reach, block = live[0, q], recv[0, q]
        return [
            total + jnp.where(lane < jnp.where(block == i, reach, 0), term, 0.0)
            for i, total in enumerate(sums)
        ]

    def column(row, start, rows):
        at = lax.broadcasted_iota(jnp.int32, (rows, WIDE), 1) == start + lax.broadcasted_iota(jnp.int32, (rows, WIDE), 0)
        picked = jnp.where(at, row, jnp.zeros_like(row))
        return jnp.broadcast_to(jnp.sum(picked, axis=1, keepdims=True), (rows, BLK))

    def nodes_of(start, rows):
        return column(node_row[...].reshape(1, WIDE).astype(jnp.float32), start, rows).astype(jnp.int32)

    def inject(total, i, nodes, gain_rows):
        return total + jnp.where(nodes == lane + (me * NB + i) * BLK, gain_rows, 0.0)

    for copy in own:
        copy.wait()

    def rows_of(total, g):
        return total[g * W : (g + 1) * W]

    def matches(nodes):
        mine = lax.broadcasted_iota(jnp.int32, (1, NET), 1) == me
        hit = jnp.zeros(nodes.shape, jnp.float32)
        for q in range(NET):
            block = jnp.sum(jnp.where(mine, meta[q].astype(jnp.float32), 0.0), axis=1, keepdims=True)
            offset = nodes - (q * NB + block.astype(jnp.int32)) * BLK
            hit = jnp.where(jnp.logical_and(offset >= 0, offset < BLK), 1.0, hit)
        return hit

    def pick(hit, there, otherwise):
        return jnp.where(hit > 0.5, there.astype(jnp.float32), otherwise.astype(jnp.float32)).astype(jnp.bfloat16)

    @pl.when(tm == 0)
    def _():
        zero[...] = jnp.zeros_like(zero)
        sums = near_terms(0, zero)
        for q in range(NET):
            sums = add_interface(sums, 0, q, zero[0])
        node_cols[...] = nodes_of(0, WIDE)
        for s in range(2):
            gain_cols[s] = column(gains[0, s : s + 1], 0, WIDE)
        for i in range(NB):
            total = inject(jnp.concatenate([sums[i]] * TM, axis=0), i, node_cols[...], gain_cols[0])
            first[i] = total.astype(jnp.bfloat16)
            for g in range(TM):
                wide_out[0, g, :, i * BLK : (i + 1) * BLK] = rows_of(total, g).astype(jnp.bfloat16)
        pltpu.make_async_copy(wide_out.at[0], out.at[0], out_recv.at[0, 0]).start()

        for i, total in enumerate(near_terms(1, first)):
            total = inject(total, i, node_cols[...], gain_cols[1])
            acc[i] = total
            for g in range(TM):
                wide[g, 0, i] = rows_of(total, g).astype(jnp.bfloat16)

        def add(q, carry):
            offset = node_cols[...] - q * NB * BLK
            inside = jnp.logical_and(offset >= 0, offset < NB * BLK)
            here = jnp.logical_and(inside, jnp.bitwise_and(offset, BLK - 1) == lane)
            values = jnp.where(here, gain_cols[0], 0.0).astype(jnp.bfloat16)
            for i, total in enumerate(add_interface([acc[i] for i in range(NB)], 1, q, values)):
                acc[i] = total
            return carry

        lax.fori_loop(0, NET, add, 0)
        for i in range(NB):
            for g in range(TM):
                wide[g, 1, i] = acc[i, g * W : (g + 1) * W].astype(jnp.bfloat16)

    pl.semaphore_wait(barrier, NET - 1 + TM - 1 + COLS - 1)

    for d in FAR:
        remote(send_hbm, meta.at[me], meta_send.at[d], meta_recv.at[d], net=lax.rem(me + d, NET)).start()

    @pl.when(tm == 0)
    def _():
        for g in range(1, TM):
            remote(wide.at[g], pair, first_send.at[g], first_recv, tm=g).start()
        pair[...] = wide[0]

    def part(t, k, kind):
        return ja.at[t, k] if kind == 0 else ia.at[t, pl.ds(k * Q, Q)]

    def whole(t, kind):
        return ja.at[t] if kind == 0 else ia.at[t]

    def three_parts(kind):
        return ja.at[0, pl.ds(0, 3)] if kind == 0 else ia.at[0, pl.ds(0, 3 * Q)]

    def spread_own(t):
        s = lax.rem(t, 2)
        for d in (1, 3, 2):
            row = lax.rem(y + d, 4)
            remote(jac.at[s, x], part(t, x, 0), ysend.at[s, 0], quarter_sem.at[t, x], tm=2 * row).start()
            remote(iface.at[s, 0, pl.ds(x * Q, Q)], part(t, x, 1), ysend.at[s, 1], quarter_sem.at[t, x], tm=2 * row + 1).start()
        remote(jac.at[s], ja.at[t], sibsend.at[t, 0], sib_sem.at[t, 0], tm=sibling).start()
        remote(iface.at[s, 0], ia.at[t], sibsend.at[t, 1], sib_sem.at[t, 1], tm=sibling).start()

    def forwarding(t, act):
        for kind in range(2):
            @pl.when(jnp.logical_and(jnp.logical_and(t < STEPS, t // 4 != y), core == kind))
            def _(kind=kind):
                act(kind)

    def to_sibling(t, k, kind):
        remote(part(t, k, kind), part(t, k, kind), sibsend.at[t, kind], sib_sem.at[t, kind], tm=sibling).start()

    def forward_own_quarter(t):
        def act(kind):
            wait(part(t, x, kind), quarter_sem.at[t, x])
            for d in (1, 3, 2):
                remote(part(t, x, kind), part(t, x, kind), xsend.at[t], quarter_sem.at[t, x], cols=lax.rem(x + d, COLS)).start()
            to_sibling(t, x, kind)

        forwarding(t, act)

    def forward_other_quarters(t):
        def act(kind):
            for d in (1, 3, 2):
                k = lax.rem(x + d, COLS)
                wait(part(t, k, kind), quarter_sem.at[t, k])
                to_sibling(t, k, kind)

        forwarding(t, act)

    def from_sibling(t):
        for kind in range(2):
            here = jnp.logical_and(t // 4 != y, core != kind)
            here = jnp.logical_or(here, jnp.logical_and(t // 4 == y, t // 2 != tm))

            @pl.when(here)
            def _(kind=kind):
                wait(whole(t, kind), sib_sem.at[t, kind])

    def spread(t):
        @pl.when(jnp.logical_and(t < STEPS, t // 2 == tm))
        def _():
            spread_own(t)

    spread(2)

    for d in range(1, TM):
        there = lax.rem(tm + d, TM)
        remote(gain_hbm, gains.at[tm], gain_send.at[d], gain_recv.at[d], tm=there).start()

    def exchange(t):
        slot = lax.rem(t, 2)
        for d in FAR:
            p = lax.rem(me + d, NET)
            sbuf[slot, d] = state[send[0, p]]
            remote(sbuf.at[slot, d], rbuf.at[slot, d], ex_send.at[slot, d], ex_recv.at[slot, d], net=p).start()

    def output(t):
        there, s = t // 2, lax.rem(t, 2)

        @pl.when(there == tm)
        def _():
            pltpu.make_async_copy(stage.at[t], out.at[s, tm], out_recv.at[s, tm]).start()

        @pl.when(there != tm)
        def _():
            remote(stage.at[t], out.at[s, tm], out_send.at[t], out_recv.at[s, tm], tm=there).start()

    def sent(slot):
        for d in FAR:
            wait(sbuf.at[slot, d], ex_send.at[slot, d])

    nodes = nodes_of(tm * W, W)
    forward_own_quarter(2)
    spread(3)

    @pl.when(tm != 0)
    def _():
        wait(pair, first_recv)

    for d in FAR:
        wait(meta.at[0], meta_recv.at[d])
    hit = matches(nodes)
    for i in range(NB):
        state[i] = pick(hit, pair[1, i], pair[0, i])


    def step(t, carry):
        slot = lax.rem(t, 2)
        exchange(t)

        @pl.when(t > 2)
        def _():
            output(t - 1)
            sent(1 - slot)

        @pl.when(jnp.logical_and(t == 2, tm == 0))
        def _():
            hits = matches(node_cols[...])
            for i in range(NB):
                for g in range(TM):
                    wide_out[1, g, :, i * BLK : (i + 1) * BLK] = pick(rows_of(hits, g), wide[g, 1, i], wide[g, 0, i])
            pltpu.make_async_copy(wide_out.at[1], out.at[1], out_recv.at[1, 0]).start()

        forward_own_quarter(t + 1)
        forward_other_quarters(t)
        spread(t + 2)
        from_sibling(t)

        @pl.when(t == 2)
        def _():
            for d in range(1, TM):
                wait(gains.at[lax.rem(tm - d + TM, TM)], gain_recv.at[d])

        gain_rows = column(gains[t // 2, pl.ds(lax.rem(t, 2), 1)], tm * W, W)
        sums = [inject(total, i, nodes, gain_rows) for i, total in enumerate(near_terms(t, state))]
        sums = add_interface(sums, t, me, state[send[0, me]])
        for group in GROUPS:
            for d in group:
                wait(rbuf.at[slot, d], ex_recv.at[slot, d])
            for d in group:
                sums = add_interface(sums, t, lax.rem(me - d + NET, NET), rbuf[slot, d])
        for i in range(NB):
            new = sums[i].astype(jnp.bfloat16)
            state[i] = new
            stage[t, :, i * BLK : (i + 1) * BLK] = new
        return carry

    lax.fori_loop(2, STEPS, step, 0)
    output(STEPS - 1)
    sent((STEPS - 1) % 2)

    def drain(t, carry):
        def act(kind):
            wait(three_parts(kind), xsend.at[t])
            wait(whole(t, kind), sibsend.at[t, kind])

        forwarding(t, act)

        @pl.when(t // 2 == tm)
        def _():
            for kind in range(2):
                wait(three_parts(kind), ysend.at[lax.rem(t, 2), kind])
                wait(whole(t, kind), sibsend.at[t, kind])

        @pl.when(t // 2 != tm)
        def _():
            wait(stage.at[t], out_send.at[t])

        return carry

    lax.fori_loop(2, STEPS, drain, 0)
    @pl.when(tm != 0)
    def _():
        for s in range(2):
            for g in range(TM):
                wait(stage.at[0], out_recv.at[s, g])

    for d in range(1, TM):
        wait(gains.at[0], gain_send.at[d])

    @pl.when(tm == 0)
    def _():
        for s in range(2):
            pltpu.make_async_copy(wide_out.at[s], out.at[s], out_recv.at[s, 0]).wait()
        for g in range(1, TM):
            wait(pair, first_send.at[g])

    for d in FAR:
        wait(meta.at[0], meta_send.at[d])


def local(jac, block_cols, iface_jac, iface_send, iface_recv, iface_live, ctrl_node, ctrl_gain):
    hbm = pl.BlockSpec(memory_space=pltpu.HBM)
    dma = pltpu.SemaphoreType.DMA
    bf16, f32, i32 = jnp.bfloat16, jnp.float32, jnp.int32
    out = pl.pallas_call(
        kernel,
        out_shape=jax.ShapeDtypeStruct((2, TM, W, NB * BLK), bf16),
        in_specs=[hbm] * 8,
        out_specs=hbm,
        scratch_shapes=[
            pltpu.VMEM((STEPS, NB, 3, BLK, BLK), bf16),
            pltpu.VMEM((STEPS, NET, BLK, BLK), bf16),
            pltpu.SMEM((2, NB), i32),
            pltpu.SMEM((1, NET), i32),
            pltpu.SMEM((1, NET), i32),
            pltpu.SMEM((1, NET), i32),
            pltpu.VMEM((WIDE,), i32),
            pltpu.VMEM((TM, 2, WIDE), f32),
            pltpu.VMEM((NET, 1, NET), i32),
            pltpu.VMEM((NB, W, BLK), bf16),
            pltpu.VMEM((2, NB, W, BLK), bf16),
            pltpu.VMEM((NB, W, BLK), bf16),
            pltpu.VMEM((TM, 2, NB, W, BLK), bf16),
            pltpu.VMEM((2, TM, W, NB * BLK), bf16),
            pltpu.VMEM((WIDE, BLK), i32),
            pltpu.VMEM((2, WIDE, BLK), f32),
            pltpu.VMEM((NB, WIDE, BLK), bf16),
            pltpu.VMEM((NB, WIDE, BLK), f32),
            pltpu.VMEM((STEPS, W, NB * BLK), bf16),
            pltpu.VMEM((2, NET, W, BLK), bf16),
            pltpu.VMEM((2, NET, W, BLK), bf16),
            dma((7,)),
            dma((2, 2)),
            dma((STEPS, COLS)),
            dma((STEPS, 2)),
            dma((2, 2)),
            dma((STEPS, 2)),
            dma((STEPS,)),
            dma((TM,)),
            dma((TM,)),
            dma((NET,)),
            dma((NET,)),
            dma((TM,)),
            dma,
            dma((2, NET)),
            dma((2, NET)),
            dma((STEPS,)),
            dma((2, TM)),
        ],
        compiler_params=pltpu.CompilerParams(
            collective_id=0, has_side_effects=True, vmem_limit_bytes=60 << 20
        ),
    )(
        jac, iface_jac, block_cols.T, iface_send, iface_recv, iface_live, ctrl_node, ctrl_gain
    )
    return out.reshape(2, WIDE, NB * BLK)


def solution(mesh):
    return jax.shard_map(
        local,
        mesh=mesh,
        in_specs=(
            P("tm", "net", None, None, None),
            P("net", None),
            P("tm", "net", None, None, None),
            P("net", None),
            P("net", None),
            P("net", None),
            P("cols"),
            P("tm", "cols"),
        ),
        out_specs=P("tm", "cols", "net"),
        check_vma=False,
    )
```

```python
import jax
import jax.numpy as jnp
from jax import lax
from jax.experimental import pallas as pl
from jax.experimental.pallas import tpu as pltpu
from jax.sharding import PartitionSpec as P

MESH = pl.DeviceIdType.MESH
TM = 8
NET = 16
COLS = 4
NB = 4
BLK = 128
STEPS = 16
WIDE = 192
W = WIDE // TM
Q = NET // COLS
NEAR = sorted(range(1, NET), key=lambda d: min(d, NET - d))
FAR = NEAR[::-1]
GROUPS = (NEAR[:10], NEAR[10:])


def dot_t(x, w):
    return lax.dot_general(
        x, w, (((1,), (1,)), ((), ())), preferred_element_type=jnp.float32
    )


def kernel(
    jac, iface, bcols_hbm, send_hbm, recv_hbm, live_hbm, node_hbm, gain_hbm, out,
    ja, ia, bcols, send, recv, live, node_row, gains, meta, state, pair, zero, wide, wide_out, node_cols, gain_cols, first, acc, stage, sbuf, rbuf,
    small_sem, own_sem, quarter_sem, sib_sem, ysend, sibsend, xsend,
    gain_send, gain_recv, meta_send, meta_recv, first_send, first_recv,
    ex_send, ex_recv, out_send, out_recv,
):
    tm = lax.axis_index("tm")
    me = lax.axis_index("net")
    x = lax.axis_index("cols")
    y, core = tm // 2, lax.rem(tm, 2)
    sibling = 2 * y + 1 - core
    lane = lax.broadcasted_iota(jnp.int32, (1, BLK), 1)

    def remote(src, dst, ssem, rsem, **device):
        return pltpu.make_async_remote_copy(
            src_ref=src, dst_ref=dst, send_sem=ssem, recv_sem=rsem,
            device_id=device, device_id_type=MESH,
        )

    def wait(ref, sem):
        pltpu.make_async_copy(ref, ref, sem).wait()

    barrier = pltpu.get_barrier_semaphore()
    for d in FAR:
        pl.semaphore_signal(barrier, inc=1, device_id={"net": lax.rem(me + d, NET)}, device_id_type=MESH)
    for d in range(1, TM):
        pl.semaphore_signal(barrier, inc=1, device_id={"tm": lax.rem(tm + d, TM)}, device_id_type=MESH)
    for d in range(1, COLS):
        pl.semaphore_signal(barrier, inc=1, device_id={"cols": lax.rem(x + d, COLS)}, device_id_type=MESH)

    own = [
        pltpu.make_async_copy(src, dst, small_sem.at[n])
        for n, (src, dst) in enumerate((
            (bcols_hbm, bcols), (send_hbm, send), (recv_hbm, recv), (live_hbm, live),
            (node_hbm, node_row), (gain_hbm, gains.at[tm]), (send_hbm, meta.at[me]),
        ))
    ]
    for s in range(2):
        own.append(pltpu.make_async_copy(jac.at[s], ja.at[2 * tm + s], own_sem.at[s, 0]))
        own.append(pltpu.make_async_copy(iface.at[s, 0], ia.at[2 * tm + s], own_sem.at[s, 1]))
    for copy in own:
        copy.start()

    def near_terms(t, ref):
        sums = []
        for i in range(NB):
            values = jnp.concatenate([ref[i], ref[bcols[0, i]], ref[bcols[1, i]]], axis=1)
            weights = jnp.concatenate([ja[t, i, 0], ja[t, i, 1], ja[t, i, 2]], axis=1)
            sums.append(dot_t(values, weights))
        return sums

    def add_interface(sums, t, q, values):
        term = dot_t(values, ia[t, q])
        reach, block = live[0, q], recv[0, q]
        return [
            total + jnp.where(lane < jnp.where(block == i, reach, 0), term, 0.0)
            for i, total in enumerate(sums)
        ]

    def column(row, start, rows):
        at = lax.broadcasted_iota(jnp.int32, (rows, WIDE), 1) == start + lax.broadcasted_iota(jnp.int32, (rows, WIDE), 0)
        picked = jnp.where(at, row, jnp.zeros_like(row))
        return jnp.broadcast_to(jnp.sum(picked, axis=1, keepdims=True), (rows, BLK))

    def nodes_of(start, rows):
        return column(node_row[...].reshape(1, WIDE).astype(jnp.float32), start, rows).astype(jnp.int32)

    def inject(total, i, nodes, gain_rows):
        return total + jnp.where(nodes == lane + (me * NB + i) * BLK, gain_rows, 0.0)

    def own_arrived():
        for copy in own:
            copy.wait()

    pl.when(tm == 0)(own_arrived)

    def rows_of(total, g):
        return total[g * W : (g + 1) * W]

    def matches(nodes):
        mine = lax.broadcasted_iota(jnp.int32, (1, NET), 1) == me
        hit = jnp.zeros(nodes.shape, jnp.float32)
        for q in range(NET):
            block = jnp.sum(jnp.where(mine, meta[q].astype(jnp.float32), 0.0), axis=1, keepdims=True)
            offset = nodes - (q * NB + block.astype(jnp.int32)) * BLK
            hit = jnp.where(jnp.logical_and(offset >= 0, offset < BLK), 1.0, hit)
        return hit

    def pick(hit, there, otherwise):
        return jnp.where(hit > 0.5, there.astype(jnp.float32), otherwise.astype(jnp.float32)).astype(jnp.bfloat16)

    @pl.when(tm == 0)
    def _():
        zero[...] = jnp.zeros_like(zero)
        sums = near_terms(0, zero)
        for q in range(NET):
            sums = add_interface(sums, 0, q, zero[0])
        node_cols[...] = nodes_of(0, WIDE)
        for s in range(2):
            gain_cols[s] = column(gains[0, s : s + 1], 0, WIDE)
        for i in range(NB):
            total = inject(jnp.concatenate([sums[i]] * TM, axis=0), i, node_cols[...], gain_cols[0])
            first[i] = total.astype(jnp.bfloat16)
            for g in range(TM):
                wide_out[0, g, :, i * BLK : (i + 1) * BLK] = rows_of(total, g).astype(jnp.bfloat16)
        pltpu.make_async_copy(wide_out.at[0], out.at[0], out_recv.at[0, 0]).start()

        for i, total in enumerate(near_terms(1, first)):
            total = inject(total, i, node_cols[...], gain_cols[1])
            acc[i] = total
            for g in range(TM):
                wide[g, 0, i] = rows_of(total, g).astype(jnp.bfloat16)

        def add(q, carry):
            offset = node_cols[...] - q * NB * BLK
            inside = jnp.logical_and(offset >= 0, offset < NB * BLK)
            here = jnp.logical_and(inside, jnp.bitwise_and(offset, BLK - 1) == lane)
            values = jnp.where(here, gain_cols[0], 0.0).astype(jnp.bfloat16)
            for i, total in enumerate(add_interface([acc[i] for i in range(NB)], 1, q, values)):
                acc[i] = total
            return carry

        lax.fori_loop(0, NET, add, 0)
        for i in range(NB):
            for g in range(TM):
                wide[g, 1, i] = acc[i, g * W : (g + 1) * W].astype(jnp.bfloat16)

    pl.semaphore_wait(barrier, NET - 1 + TM - 1 + COLS - 1)

    for d in FAR:
        remote(send_hbm, meta.at[me], meta_send.at[d], meta_recv.at[d], net=lax.rem(me + d, NET)).start()

    @pl.when(tm == 0)
    def _():
        for g in range(1, TM):
            remote(wide.at[g], pair, first_send.at[g], first_recv, tm=g).start()
        pair[...] = wide[0]

    def part(t, k, kind):
        return ja.at[t, k] if kind == 0 else ia.at[t, pl.ds(k * Q, Q)]

    def whole(t, kind):
        return ja.at[t] if kind == 0 else ia.at[t]

    def three_parts(kind):
        return ja.at[0, pl.ds(0, 3)] if kind == 0 else ia.at[0, pl.ds(0, 3 * Q)]

    def spread_own(t):
        s = lax.rem(t, 2)
        for d in (1, 3, 2):
            row = lax.rem(y + d, 4)
            remote(jac.at[s, x], part(t, x, 0), ysend.at[s, 0], quarter_sem.at[t, x], tm=2 * row).start()
            remote(iface.at[s, 0, pl.ds(x * Q, Q)], part(t, x, 1), ysend.at[s, 1], quarter_sem.at[t, x], tm=2 * row + 1).start()
        remote(jac.at[s], ja.at[t], sibsend.at[t, 0], sib_sem.at[t, 0], tm=sibling).start()
        remote(iface.at[s, 0], ia.at[t], sibsend.at[t, 1], sib_sem.at[t, 1], tm=sibling).start()

    def forwarding(t, act):
        for kind in range(2):
            @pl.when(jnp.logical_and(jnp.logical_and(t < STEPS, t // 4 != y), core == kind))
            def _(kind=kind):
                act(kind)

    def to_sibling(t, k, kind):
        remote(part(t, k, kind), part(t, k, kind), sibsend.at[t, kind], sib_sem.at[t, kind], tm=sibling).start()

    def forward_own_quarter(t):
        def act(kind):
            wait(part(t, x, kind), quarter_sem.at[t, x])
            for d in (1, 3, 2):
                remote(part(t, x, kind), part(t, x, kind), xsend.at[t], quarter_sem.at[t, x], cols=lax.rem(x + d, COLS)).start()
            to_sibling(t, x, kind)

        forwarding(t, act)

    def forward_other_quarters(t):
        def act(kind):
            for d in (1, 3, 2):
                k = lax.rem(x + d, COLS)
                wait(part(t, k, kind), quarter_sem.at[t, k])
                to_sibling(t, k, kind)

        forwarding(t, act)

    def from_sibling(t):
        for kind in range(2):
            here = jnp.logical_and(t // 4 != y, core != kind)
            here = jnp.logical_or(here, jnp.logical_and(t // 4 == y, t // 2 != tm))

            @pl.when(here)
            def _(kind=kind):
                wait(whole(t, kind), sib_sem.at[t, kind])

    def spread(t):
        @pl.when(jnp.logical_and(t < STEPS, t // 2 == tm))
        def _():
            spread_own(t)

    spread(2)

    for d in range(1, TM):
        there = lax.rem(tm + d, TM)
        remote(gain_hbm, gains.at[tm], gain_send.at[d], gain_recv.at[d], tm=there).start()

    def exchange(t):
        slot = lax.rem(t, 2)
        for d in FAR:
            p = lax.rem(me + d, NET)
            sbuf[slot, d] = state[send[0, p]]
            remote(sbuf.at[slot, d], rbuf.at[slot, d], ex_send.at[slot, d], ex_recv.at[slot, d], net=p).start()

    def output(t):
        there, s = t // 2, lax.rem(t, 2)

        @pl.when(there == tm)
        def _():
            pltpu.make_async_copy(stage.at[t], out.at[s, tm], out_recv.at[s, tm]).start()

        @pl.when(there != tm)
        def _():
            remote(stage.at[t], out.at[s, tm], out_send.at[t], out_recv.at[s, tm], tm=there).start()

    def sent(slot):
        for d in FAR:
            wait(sbuf.at[slot, d], ex_send.at[slot, d])

    pl.when(tm != 0)(own_arrived)
    nodes = nodes_of(tm * W, W)
    forward_own_quarter(2)
    spread(3)

    @pl.when(tm != 0)
    def _():
        wait(pair, first_recv)

    for d in FAR:
        wait(meta.at[0], meta_recv.at[d])
    hit = matches(nodes)
    for i in range(NB):
        state[i] = pick(hit, pair[1, i], pair[0, i])


    def step(t, carry):
        slot = lax.rem(t, 2)
        exchange(t)

        @pl.when(t > 2)
        def _():
            output(t - 1)
            sent(1 - slot)

        @pl.when(jnp.logical_and(t == 2, tm == 0))
        def _():
            hits = matches(node_cols[...])
            for i in range(NB):
                for g in range(TM):
                    wide_out[1, g, :, i * BLK : (i + 1) * BLK] = pick(rows_of(hits, g), wide[g, 1, i], wide[g, 0, i])
            pltpu.make_async_copy(wide_out.at[1], out.at[1], out_recv.at[1, 0]).start()

        forward_own_quarter(t + 1)
        forward_other_quarters(t)
        spread(t + 2)
        from_sibling(t)

        @pl.when(t == 2)
        def _():
            for d in range(1, TM):
                wait(gains.at[lax.rem(tm - d + TM, TM)], gain_recv.at[d])

        gain_rows = column(gains[t // 2, pl.ds(lax.rem(t, 2), 1)], tm * W, W)
        sums = [inject(total, i, nodes, gain_rows) for i, total in enumerate(near_terms(t, state))]
        sums = add_interface(sums, t, me, state[send[0, me]])
        for group in GROUPS:
            for d in group:
                wait(rbuf.at[slot, d], ex_recv.at[slot, d])
            for d in group:
                sums = add_interface(sums, t, lax.rem(me - d + NET, NET), rbuf[slot, d])
        for i in range(NB):
            new = sums[i].astype(jnp.bfloat16)
            state[i] = new
            stage[t, :, i * BLK : (i + 1) * BLK] = new
        return carry

    lax.fori_loop(2, STEPS, step, 0)
    output(STEPS - 1)
    sent((STEPS - 1) % 2)

    def drain(t, carry):
        def act(kind):
            wait(three_parts(kind), xsend.at[t])
            wait(whole(t, kind), sibsend.at[t, kind])

        forwarding(t, act)

        @pl.when(t // 2 == tm)
        def _():
            for kind in range(2):
                wait(three_parts(kind), ysend.at[lax.rem(t, 2), kind])
                wait(whole(t, kind), sibsend.at[t, kind])

        @pl.when(t // 2 != tm)
        def _():
            wait(stage.at[t], out_send.at[t])

        return carry

    lax.fori_loop(2, STEPS, drain, 0)
    @pl.when(tm != 0)
    def _():
        for s in range(2):
            for g in range(TM):
                wait(stage.at[0], out_recv.at[s, g])

    for d in range(1, TM):
        wait(gains.at[0], gain_send.at[d])

    @pl.when(tm == 0)
    def _():
        for s in range(2):
            pltpu.make_async_copy(wide_out.at[s], out.at[s], out_recv.at[s, 0]).wait()
        for g in range(1, TM):
            wait(pair, first_send.at[g])

    for d in FAR:
        wait(meta.at[0], meta_send.at[d])


def local(jac, block_cols, iface_jac, iface_send, iface_recv, iface_live, ctrl_node, ctrl_gain):
    hbm = pl.BlockSpec(memory_space=pltpu.HBM)
    dma = pltpu.SemaphoreType.DMA
    bf16, f32, i32 = jnp.bfloat16, jnp.float32, jnp.int32
    out = pl.pallas_call(
        kernel,
        out_shape=jax.ShapeDtypeStruct((2, TM, W, NB * BLK), bf16),
        in_specs=[hbm] * 8,
        out_specs=hbm,
        scratch_shapes=[
            pltpu.VMEM((STEPS, NB, 3, BLK, BLK), bf16),
            pltpu.VMEM((STEPS, NET, BLK, BLK), bf16),
            pltpu.SMEM((2, NB), i32),
            pltpu.SMEM((1, NET), i32),
            pltpu.SMEM((1, NET), i32),
            pltpu.SMEM((1, NET), i32),
            pltpu.VMEM((WIDE,), i32),
            pltpu.VMEM((TM, 2, WIDE), f32),
            pltpu.VMEM((NET, 1, NET), i32),
            pltpu.VMEM((NB, W, BLK), bf16),
            pltpu.VMEM((2, NB, W, BLK), bf16),
            pltpu.VMEM((NB, W, BLK), bf16),
            pltpu.VMEM((TM, 2, NB, W, BLK), bf16),
            pltpu.VMEM((2, TM, W, NB * BLK), bf16),
            pltpu.VMEM((WIDE, BLK), i32),
            pltpu.VMEM((2, WIDE, BLK), f32),
            pltpu.VMEM((NB, WIDE, BLK), bf16),
            pltpu.VMEM((NB, WIDE, BLK), f32),
            pltpu.VMEM((STEPS, W, NB * BLK), bf16),
            pltpu.VMEM((2, NET, W, BLK), bf16),
            pltpu.VMEM((2, NET, W, BLK), bf16),
            dma((7,)),
            dma((2, 2)),
            dma((STEPS, COLS)),
            dma((STEPS, 2)),
            dma((2, 2)),
            dma((STEPS, 2)),
            dma((STEPS,)),
            dma((TM,)),
            dma((TM,)),
            dma((NET,)),
            dma((NET,)),
            dma((TM,)),
            dma,
            dma((2, NET)),
            dma((2, NET)),
            dma((STEPS,)),
            dma((2, TM)),
        ],
        compiler_params=pltpu.CompilerParams(
            collective_id=0, has_side_effects=True, vmem_limit_bytes=60 << 20
        ),
    )(
        jac, iface_jac, block_cols.T, iface_send, iface_recv, iface_live, ctrl_node, ctrl_gain
    )
    return out.reshape(2, WIDE, NB * BLK)


def solution(mesh):
    return jax.shard_map(
        local,
        mesh=mesh,
        in_specs=(
            P("tm", "net", None, None, None),
            P("net", None),
            P("tm", "net", None, None, None),
            P("net", None),
            P("net", None),
            P("net", None),
            P("cols"),
            P("tm", "cols"),
        ),
        out_specs=P("tm", "cols", "net"),
        check_vma=False,
    )
```
